128 devices in a mesh: row: 16 (over y_lo, z, core), col: 8 (over x, y_hi).
Axes of the slice: x: 4, y: 4 (y_hi: 2, y_lo: 2; y = y_hi * 2 + y_lo), z: 4, core: 2. Of those that a mesh axis runs over, the one named last changes fastest.
Arguments:
- hidden_in: bfloat16 [8192, 2048], P('row'), may hold values from -6 to 6
- gain_attn: float32 [2048], replicated, may hold values from 0.1 to 1.9
- gain_mlp: float32 [2048], replicated, may hold values from 0.1 to 1.9
- w_qkv: bfloat16 [2048, 3, 2048], P('row', None, 'col'), may hold values from -0.25 to 0.25
- w_up: bfloat16 [2048, 8192], P('row', 'col'), may hold values from -0.25 to 0.25
- w_out: bfloat16 [2048, 2048], P('col', 'row'), may hold values from -0.125 to 0.125
- w_down: bfloat16 [8192, 2048], P('col', 'row'), may hold values from -0.0625 to 0.0625
- prefix_cache: bfloat16 [128, 128, 2, 2048], P('row', None, None, 'col'), may hold values from -136 to 136, as said below
- suffix_lengths: int32 [64], replicated, may hold values from 1 to 512, 8192 in all
- cached_lengths: int32 [64], replicated, may hold values from 1 to 8192, as said below
- request_group: int32 [64], replicated, may hold values from 0 to 1
- page_table: int32 [128], replicated, may hold values from 0 to 127, each once
Outputs:
- hidden_out: bfloat16 [8192, 2048], P('row', 'col')
- suffix_keys: bfloat16 [8192, 2048], P('row', 'col')
- suffix_values: bfloat16 [8192, 2048], P('row', 'col')
The draws below stay inside these ranges and needn't reach their ends.
Inputs may be any that keep to these rules, and one draw needn't show every extreme that they name: `suffix_lengths`: the lengths sum to 8192; some request has exactly 512 tokens. `cached_lengths`: some request reuses all 8192 tokens of its prefix. `page_table`: each slot appears once; slot s is held by index s // 8 of row. `prefix_cache`: keys and values of the prefix pages.
All inputs are finite; a program needn't handle non-finite values.
Results may differ from the reference program's by a relative error of at most 0.02.
Values may be sent and summed in bfloat16 or wider, within the bound.
A program may use at most 128 MiB of HBM per device.

```python
import math
import jax
import jax.numpy as jnp
import numpy as np
from jax import lax

D = 2048
HEADS = 8
HD = 256
FF = 8192
ROT = 64
PAGE = 128
GROUPS = 2
SUF_DEV = 512
TOKENS = 8192
REQS = 64
PAGES = 128
PREF = 8192
N_ROW = 16


def draw_prefix_cache(key, part):
    shape = (PAGES, PAGE, 2, D)
    return (2.0 * jax.random.truncated_normal(key, -6.0, 6.0, shape, jnp.float32)).astype(jnp.bfloat16)


def draw_cached_lengths(key, part):
    first, second = jax.random.split(key)
    values = jax.random.randint(first, (REQS,), 1, PREF + 1)
    spot = jax.random.randint(second, (), 0, REQS)
    return jnp.where(jnp.arange(REQS) == spot, PREF, values).astype(jnp.int32)


def place_ends(result, own_key, smallest, high):
    spot = [jax.random.randint(jax.random.fold_in(own_key, axis), (), 0, length) for axis, length in enumerate(result.shape)]
    main_axis = result.shape.index(max(result.shape))
    next_to = spot[:main_axis] + [(spot[main_axis] + 1) % result.shape[main_axis]] + spot[main_axis + 1:]
    return result.at[tuple(spot)].set(smallest).at[tuple(next_to)].set(high)


def block_scale(rng, extent, pieces, smallest, top_value):
    gain, own = 1.0, jax.random.fold_in(rng, 6)
    for dim, shards_of in pieces:
        draws = jnp.exp(jax.random.uniform(jax.random.fold_in(own, dim), (shards_of,), jnp.float32, smallest / len(pieces), top_value / len(pieces)))
        gain = gain * jnp.repeat(draws, extent[dim] // shards_of).reshape([-1 if axis == dim else 1 for axis in range(len(extent))])
    return gain


def length_profile(count, total, most, skew):
    portions = [(1 << 20) // math.isqrt(grade ** skew) + 1 for grade in range(2, count + 1)]
    surplus, holding = total - most - (count - 1), [1] * (count - 1)
    while surplus > 0:
        movable = [i for i in range(count - 1) if holding[i] < most]
        pool, left = sum([portions[i] for i in movable]), surplus
        for i in movable:
            extra = min(most - holding[i], max(1, left * portions[i] // pool), surplus)
            holding[i] = holding[i] + extra
            surplus = surplus - extra
    return np.array([most] + holding)


def ragged(own_key, count, total, most, skew):
    if count == 2:
        one = jax.random.randint(own_key, (), max(1, total - most), min(most, total - 1) + 1)
        return jnp.stack([one, total - one])
    lengths = jnp.asarray(length_profile(count, total, most, skew), jnp.int32)
    couples = (count - 1) // 2
    donor, receiver = lengths[1:1 + 2 * couples:2], lengths[2:2 + 2 * couples:2]
    slack = jnp.minimum(donor - 1, most - receiver)
    shifted = jax.random.randint(jax.random.fold_in(own_key, 1), (couples,), 0, 1 << 20) % (slack + 1)
    lengths = lengths.at[1:1 + 2 * couples:2].set(donor - shifted).at[2:2 + 2 * couples:2].set(receiver + shifted)
    return lengths[jax.random.permutation(jax.random.fold_in(own_key, 2), count)]


def gaussian(stream_key, extent, scale, most, cuts=(), kind=jnp.bfloat16):
    drawn = jax.random.normal(stream_key, extent, jnp.float32) * scale
    if len(cuts) > 0:
        drawn = block_scale(stream_key, extent, cuts, -0.22, 0.18) * drawn
    return jnp.clip(drawn, min=-most, max=most).astype(kind)


def setup_inputs(seed: int = 0) -> dict:
    streams_of = jax.random.split(jax.random.key(seed), 13)
    hidden_in = gaussian(streams_of[0], (TOKENS, D), 1.0, 6.0, ((0, 16),))
    gain_attn = jnp.clip(1.0 + 0.18 * jax.random.normal(streams_of[1], (D,), jnp.float32), 0.1, 1.9)
    gain_mlp = jnp.clip(1.0 + 0.18 * jax.random.normal(streams_of[2], (D,), jnp.float32), 0.1, 1.9)
    w_qkv = gaussian(streams_of[3], (D, 3, D), (D // 4) ** -0.5, 0.25, ((0, 16), (2, 8)))
    w_up = gaussian(streams_of[4], (D, FF), (D // 4) ** -0.5, 0.25, ((0, 16), (1, 8)))
    w_out = gaussian(streams_of[5], (D, D), D ** -0.5, 0.125, ((0, 8), (1, 16)))
    w_down = gaussian(streams_of[6], (FF, D), FF ** -0.5, 0.0625, ((0, 8), (1, 16)))
    prefix_cache = draw_prefix_cache(jax.random.fold_in(streams_of[12], 71), 0)
    suffix_lengths = ragged(streams_of[8], REQS, TOKENS, SUF_DEV, 2).astype(jnp.int32)
    cached_lengths = draw_cached_lengths(jax.random.fold_in(streams_of[12], 71), 0)
    request_group = place_ends(jax.random.randint(streams_of[10], (REQS,), 0, GROUPS), jax.random.fold_in(streams_of[10], 1), 0, GROUPS - 1).astype(jnp.int32)
    page_table = jax.random.permutation(streams_of[11], PAGES).astype(jnp.int32)
    return {"hidden_in": hidden_in, "gain_attn": gain_attn, "gain_mlp": gain_mlp, "w_qkv": w_qkv, "w_up": w_up, "w_out": w_out, "w_down": w_down, "prefix_cache": prefix_cache, "suffix_lengths": suffix_lengths, "cached_lengths": cached_lengths, "request_group": request_group, "page_table": page_table}


very_low = -1e+30
norm_epsilon = 1e-05

def layer_normalize(values):
    floats = values.astype(jnp.float32)
    average = lax.optimization_barrier(jnp.mean(floats, -1, keepdims=True))
    centered = floats - average
    spread = lax.optimization_barrier(jnp.mean(centered * centered, -1, keepdims=True))
    return centered * lax.rsqrt(spread + norm_epsilon)

def rotary(vectors, position):
    half_rot = ROT // 2
    exponent = jnp.arange(half_rot, dtype=jnp.float32) * (2.0 / ROT)
    frequency = 10000.0 ** (-exponent)
    angles = position.astype(jnp.float32)[:, None] * frequency[None, :]
    cosine = jnp.concatenate([jnp.cos(angles), jnp.cos(angles)], 1)[:, None, :]
    sine = jnp.concatenate([jnp.sin(angles), jnp.sin(angles)], 1)[:, None, :]
    rotated = vectors[..., :ROT]
    turned = jnp.concatenate([-rotated[..., half_rot:], rotated[..., :half_rot]], -1)
    return jnp.concatenate([rotated * cosine + turned * sine, vectors[..., ROT:]], -1)

def token_table(suffix_lengths, cached_lengths, request_group, count):
    starts = (jnp.cumsum(suffix_lengths, dtype=jnp.int32) - suffix_lengths).astype(jnp.int32)
    token_ids = jnp.arange(count, dtype=jnp.int32)
    request = lax.optimization_barrier(jnp.sum((starts[None, :] <= token_ids[:, None]).astype(jnp.int32), 1, dtype=jnp.int32)) - 1
    onehot = (request[:, None] == jnp.arange(suffix_lengths.shape[0], dtype=jnp.int32)[None, :]).astype(jnp.int32)
    begin = lax.optimization_barrier(jnp.sum(onehot * starts[None, :], 1, dtype=jnp.int32))
    limit = lax.optimization_barrier(jnp.sum(onehot * cached_lengths[None, :], 1, dtype=jnp.int32))
    group_of = lax.optimization_barrier(jnp.sum(onehot * request_group[None, :], 1, dtype=jnp.int32))
    return (request.astype(jnp.int32), (limit + token_ids - begin).astype(jnp.int32), group_of, limit)

def reference(hidden_in, gain_attn, gain_mlp, w_qkv, w_up, w_out, w_down, prefix_cache, suffix_lengths, cached_lengths, request_group, page_table):
    normed = layer_normalize(hidden_in)
    attn_in = (normed * gain_attn).astype(jnp.bfloat16)
    mlp_in = (normed * gain_mlp).astype(jnp.bfloat16)
    projected = jnp.dot(attn_in, w_qkv.reshape(D, 3 * D), preferred_element_type=jnp.float32).reshape(TOKENS, 3, HEADS, HD)
    request, position, group_of, limit = token_table(suffix_lengths, cached_lengths, request_group, TOKENS)
    queries = (rotary(projected[:, 0], position) * HD ** (-0.5)).astype(jnp.bfloat16)
    keys_new = rotary(projected[:, 1], position).astype(jnp.bfloat16)
    values_new = projected[:, 2].astype(jnp.bfloat16)
    logical = prefix_cache[page_table].reshape(GROUPS * PREF, 2, HEADS, HD)
    prefix_keys = logical[:, 0]
    prefix_values = logical[:, 1]
    key_group = jnp.repeat(jnp.arange(GROUPS, dtype=jnp.int32), PREF)
    key_position = jnp.tile(jnp.arange(PREF, dtype=jnp.int32), GROUPS)
    padded_keys = jnp.concatenate([jnp.zeros((SUF_DEV, HEADS, HD), jnp.bfloat16), keys_new], 0)
    padded_values = jnp.concatenate([jnp.zeros((SUF_DEV, HEADS, HD), jnp.bfloat16), values_new], 0)
    padded_request = jnp.concatenate([jnp.full((SUF_DEV,), -1, jnp.int32), request], 0)

    def one_block(block):
        first = (block * SUF_DEV).astype(jnp.int32)
        token_ids = first + jnp.arange(SUF_DEV, dtype=jnp.int32)
        window_ids = first - SUF_DEV + jnp.arange(2 * SUF_DEV, dtype=jnp.int32)
        query_block = lax.dynamic_slice_in_dim(queries, first, SUF_DEV, 0)
        query_request = lax.dynamic_slice_in_dim(request, first, SUF_DEV, 0)
        query_group = lax.dynamic_slice_in_dim(group_of, first, SUF_DEV, 0)
        query_limit = lax.dynamic_slice_in_dim(limit, first, SUF_DEV, 0)
        window_keys = lax.dynamic_slice_in_dim(padded_keys, first, 2 * SUF_DEV, 0)
        window_values = lax.dynamic_slice_in_dim(padded_values, first, 2 * SUF_DEV, 0)
        window_request = lax.dynamic_slice_in_dim(padded_request, first, 2 * SUF_DEV, 0)
        visible_prefix = (key_group[None, :] == query_group[:, None]) & (key_position[None, :] < query_limit[:, None])
        visible_suffix = (window_request[None, :] == query_request[:, None]) & (window_ids[None, :] <= token_ids[:, None])
        visible = jnp.concatenate([visible_prefix, visible_suffix], 1)
        all_keys = jnp.concatenate([prefix_keys, window_keys], 0)
        all_values = jnp.concatenate([prefix_values, window_values], 0)

        def one_head(head):
            scores = jnp.dot(query_block[:, head], all_keys[:, head].T, preferred_element_type=jnp.float32)
            peak = lax.optimization_barrier(jnp.max(jnp.where(visible, scores, very_low), 1, keepdims=True))
            weights = jnp.where(visible, jnp.exp(scores - peak), 0.0)
            total = lax.optimization_barrier(jnp.sum(weights, 1, keepdims=True))
            mixed = jnp.dot(weights.astype(jnp.bfloat16), all_values[:, head], preferred_element_type=jnp.float32) / total
            return mixed.astype(jnp.bfloat16)
        per_head = lax.map(one_head, jnp.arange(HEADS, dtype=jnp.int32))
        return jnp.transpose(per_head, (1, 0, 2)).reshape(SUF_DEV, D)
    attention = lax.map(one_block, jnp.arange(N_ROW, dtype=jnp.int32)).reshape(TOKENS, D)
    activated = jax.nn.gelu(jnp.dot(mlp_in, w_up, preferred_element_type=jnp.float32), approximate=False).astype(jnp.bfloat16)
    summed = jnp.dot(attention, w_out, preferred_element_type=jnp.float32) + jnp.dot(activated, w_down, preferred_element_type=jnp.float32)
    hidden_out = (hidden_in.astype(jnp.float32) + summed).astype(jnp.bfloat16)
    return (hidden_out, keys_new.reshape(TOKENS, D), values_new.reshape(TOKENS, D))
```

```python
import math

import jax
import jax.numpy as jnp
from jax import lax
from jax.sharding import PartitionSpec as P

HD = 256
ROT = 64
PAGE = 128
GROUPS = 2


very_low = -1e30
norm_epsilon = 1e-05


def from_behind(block, axis, distance):
    devices = range(lax.axis_size(axis))
    route = [(i - distance, i) for i in devices if i - distance in devices]
    return lax.ppermute(block, axis, route)


def layer_normalize(values):
    floats = values.astype(jnp.float32)
    average = jnp.mean(floats, -1, keepdims=True)
    centered = floats - average
    spread = jnp.mean(centered * centered, -1, keepdims=True)
    return centered * lax.rsqrt(spread + norm_epsilon)


def rotary(vectors, position):
    half_rot = ROT // 2
    exponent = jnp.arange(half_rot, dtype=jnp.float32) * (2.0 / ROT)
    frequency = 10000.0 ** (-exponent)
    angles = position.astype(jnp.float32)[:, None] * frequency[None, :]
    cosine = jnp.concatenate([jnp.cos(angles), jnp.cos(angles)], 1)[:, None, :]
    sine = jnp.concatenate([jnp.sin(angles), jnp.sin(angles)], 1)[:, None, :]
    rotated = vectors[..., :ROT]
    turned = jnp.concatenate([-rotated[..., half_rot:], rotated[..., :half_rot]], -1)
    return jnp.concatenate([rotated * cosine + turned * sine, vectors[..., ROT:]], -1)


def token_table(suffix_lengths, cached_lengths, request_group, count):
    starts = jnp.cumsum(suffix_lengths, dtype=jnp.int32) - suffix_lengths
    token_ids = jnp.arange(count, dtype=jnp.int32)
    request = (
        jnp.sum((starts[None, :] <= token_ids[:, None]).astype(jnp.int32), 1, dtype=jnp.int32) - 1
    )
    onehot = (
        request[:, None] == jnp.arange(suffix_lengths.shape[0], dtype=jnp.int32)[None, :]
    ).astype(jnp.int32)
    begin = jnp.sum(onehot * starts[None, :], 1, dtype=jnp.int32)
    limit = jnp.sum(onehot * cached_lengths[None, :], 1, dtype=jnp.int32)
    group_of = jnp.sum(onehot * request_group[None, :], 1, dtype=jnp.int32)
    return (request, limit + token_ids - begin, group_of, limit)


def partial_softmax(scores, visible, value_block):
    allowed = visible[None, :, :]
    peak = jnp.max(jnp.where(allowed, scores, very_low), -1)
    weights = jnp.where(allowed, jnp.exp(scores - peak[..., None]), 0.0)
    total = jnp.sum(weights, -1)
    mixed = jnp.einsum(
        "hqk,khe->qhe",
        weights.astype(jnp.bfloat16),
        value_block,
        preferred_element_type=jnp.float32,
    )
    return (peak, total, mixed)


def combine(earlier, later):
    peak = jnp.maximum(earlier[0], later[0])
    scale_one = jnp.exp(earlier[0] - peak)
    scale_two = jnp.exp(later[0] - peak)
    total = earlier[1] * scale_one + later[1] * scale_two
    mixed = earlier[2] * scale_one.T[:, :, None] + later[2] * scale_two.T[:, :, None]
    return (peak, total, mixed)


def prefix_fold(running, cache_rows, query_block, query_group, query_limit, page_table):
    count = cache_rows.shape[0]
    stride = math.gcd(count, 8)
    heads_here = query_block.shape[1]
    per_prefix = page_table.shape[0] // GROUPS
    table_index = jnp.arange(page_table.shape[0], dtype=jnp.int32)

    def advance(turn_index, inner):
        block_rows = lax.dynamic_slice_in_dim(cache_rows, turn_index * stride, stride, 0)
        slots = turn_index * stride + jnp.arange(stride, dtype=jnp.int32)
        logical = jnp.sum(
            table_index[None, :] * (page_table[None, :] == slots[:, None]).astype(jnp.int32),
            1,
            dtype=jnp.int32,
        )
        key_group = jnp.repeat(logical // per_prefix, PAGE)
        key_position = (
            (logical % per_prefix)[:, None] * PAGE + jnp.arange(PAGE, dtype=jnp.int32)[None, :]
        ).reshape(-1)
        key_block = block_rows[:, :, 0].reshape(stride * PAGE, heads_here, HD)
        value_block = block_rows[:, :, 1].reshape(stride * PAGE, heads_here, HD)
        visible = (key_group[None, :] == query_group[:, None]) & (
            key_position[None, :] < query_limit[:, None]
        )
        scores = jnp.einsum(
            "qhe,khe->hqk", query_block, key_block, preferred_element_type=jnp.float32
        )
        return combine(inner, partial_softmax(scores, visible, value_block))

    return lax.fori_loop(0, count // stride, advance, running)


def body(
    hidden_in,
    gain_attn,
    gain_mlp,
    w_qkv,
    w_up,
    w_out,
    w_down,
    prefix_cache,
    suffix_lengths,
    cached_lengths,
    request_group,
    page_table,
):
    row_count = hidden_in.shape[0]
    model_width = hidden_in.shape[1]
    row_total = lax.axis_size("row")
    col_total = lax.axis_size("col")
    row_place = lax.axis_index("row")
    col_place = lax.axis_index("col")
    head_width = w_qkv.shape[2]
    heads_here = head_width // HD
    normed = layer_normalize(hidden_in)
    attn_in = (normed * gain_attn).astype(jnp.bfloat16)
    mlp_in = (normed * gain_mlp).astype(jnp.bfloat16)
    rows_here = w_qkv.shape[0]
    qkv_columns = 3 * head_width
    joined = jnp.concatenate([w_qkv.reshape(rows_here, qkv_columns), w_up], 1)
    joined = lax.all_gather(joined, "row", axis=0, tiled=True)
    qkv_all = joined[:, :qkv_columns].reshape(model_width, 3, head_width)
    projected = jnp.einsum("td,dkh->tkh", attn_in, qkv_all, preferred_element_type=jnp.float32)
    up_sum = jnp.dot(mlp_in, joined[:, qkv_columns:], preferred_element_type=jnp.float32)
    token_total = row_total * row_count
    request_all, position_all, group_all, limit_all = token_table(
        suffix_lengths, cached_lengths, request_group, token_total
    )
    first_row = row_place * row_count
    local_request = lax.dynamic_slice_in_dim(request_all, first_row, row_count, 0)
    local_position = lax.dynamic_slice_in_dim(position_all, first_row, row_count, 0)
    local_group = lax.dynamic_slice_in_dim(group_all, first_row, row_count, 0)
    local_limit = lax.dynamic_slice_in_dim(limit_all, first_row, row_count, 0)
    projected = projected.reshape(row_count, 3, heads_here, HD)
    queries = (rotary(projected[:, 0], local_position) * HD ** (-0.5)).astype(jnp.bfloat16)
    keys_flat = (
        rotary(projected[:, 1], local_position).astype(jnp.bfloat16).reshape(row_count, head_width)
    )
    values_flat = projected[:, 2].astype(jnp.bfloat16).reshape(row_count, head_width)
    pair_rows = jnp.stack([keys_flat, values_flat], 1)
    previous = from_behind(pair_rows, "row", 1)
    window = jnp.concatenate([previous, pair_rows], 0)
    window_ids = first_row - row_count + jnp.arange(2 * row_count, dtype=jnp.int32)
    padded_request = jnp.concatenate([jnp.full((row_count,), -1, jnp.int32), request_all], 0)
    window_request = lax.dynamic_slice_in_dim(padded_request, first_row, 2 * row_count, 0)
    token_ids = first_row + jnp.arange(row_count, dtype=jnp.int32)
    visible = (window_request[None, :] == local_request[:, None]) & (
        window_ids[None, :] <= token_ids[:, None]
    )
    window_keys = window[:, 0].reshape(2 * row_count, heads_here, HD)
    window_values = window[:, 1].reshape(2 * row_count, heads_here, HD)
    scores = jnp.einsum("qhe,khe->hqk", queries, window_keys, preferred_element_type=jnp.float32)
    suffix_state = partial_softmax(scores, visible, window_values)
    start_state = (
        jnp.full((heads_here, row_count), very_low, jnp.float32),
        jnp.zeros((heads_here, row_count), jnp.float32),
        jnp.zeros((row_count, heads_here, HD), jnp.float32),
    )
    prefix_state = prefix_fold(
        start_state,
        lax.all_gather(prefix_cache, "row", axis=0, tiled=True),
        queries,
        local_group,
        local_limit,
        page_table,
    )
    final = combine(prefix_state, suffix_state)
    attention = (
        (final[2] / final[1].T[:, :, None]).astype(jnp.bfloat16).reshape(row_count, head_width)
    )
    activated = jax.nn.gelu(up_sum, approximate=False).astype(jnp.bfloat16)
    out_rows = w_out.shape[0]
    joined = jnp.concatenate([w_out.T, w_down.T], 1)
    joined = lax.all_gather(joined, "row", axis=0, tiled=True)
    contribution = jnp.einsum(
        "th,dh->td", attention, joined[:, :out_rows], preferred_element_type=jnp.float32
    ) + jnp.einsum("tf,df->td", activated, joined[:, out_rows:], preferred_element_type=jnp.float32)
    summed = lax.psum_scatter(
        contribution.astype(jnp.bfloat16), "col", scatter_dimension=1, tiled=True
    ).astype(jnp.float32)
    share = model_width // col_total
    residual = lax.dynamic_slice_in_dim(hidden_in, col_place * share, share, 1).astype(jnp.float32)
    return ((residual + summed).astype(jnp.bfloat16), keys_flat, values_flat)


def solution(mesh):
    in_specs = (
        P("row", None),
        P(),
        P(),
        P("row", None, "col"),
        P("row", "col"),
        P("col", "row"),
        P("col", "row"),
        P("row", None, None, "col"),
        P(),
        P(),
        P(),
        P(),
    )
    out_specs = (P("row", "col"), P("row", "col"), P("row", "col"))
    return jax.shard_map(body, mesh=mesh, in_specs=in_specs, out_specs=out_specs, check_vma=False)
```

```python
import functools
import math

import jax
import jax.numpy as jnp
from jax import lax
from jax.experimental import pallas as pl
from jax.experimental.pallas import tpu as pltpu
from jax.sharding import PartitionSpec as P

HD = 256
ROT = 64
PAGE = 128
GROUPS = 2


very_low = -1e30
norm_epsilon = 1e-05


def from_behind(block, axis, distance):
    devices = range(lax.axis_size(axis))
    route = [(i - distance, i) for i in devices if i - distance in devices]
    return lax.ppermute(block, axis, route)


def layer_normalize(values):
    floats = values.astype(jnp.float32)
    average = jnp.mean(floats, -1, keepdims=True)
    centered = floats - average
    spread = jnp.mean(centered * centered, -1, keepdims=True)
    return centered * lax.rsqrt(spread + norm_epsilon)


def rotary(vectors, position):
    half_rot = ROT // 2
    exponent = jnp.arange(half_rot, dtype=jnp.float32) * (2.0 / ROT)
    frequency = 10000.0 ** (-exponent)
    angles = position.astype(jnp.float32)[:, None] * frequency[None, :]
    cosine = jnp.concatenate([jnp.cos(angles), jnp.cos(angles)], 1)[:, None, :]
    sine = jnp.concatenate([jnp.sin(angles), jnp.sin(angles)], 1)[:, None, :]
    rotated = vectors[..., :ROT]
    turned = jnp.concatenate([-rotated[..., half_rot:], rotated[..., :half_rot]], -1)
    return jnp.concatenate([rotated * cosine + turned * sine, vectors[..., ROT:]], -1)


def token_table(suffix_lengths, cached_lengths, request_group, count):
    starts = jnp.cumsum(suffix_lengths, dtype=jnp.int32) - suffix_lengths
    token_ids = jnp.arange(count, dtype=jnp.int32)
    request = (
        jnp.sum((starts[None, :] <= token_ids[:, None]).astype(jnp.int32), 1, dtype=jnp.int32) - 1
    )
    onehot = (
        request[:, None] == jnp.arange(suffix_lengths.shape[0], dtype=jnp.int32)[None, :]
    ).astype(jnp.int32)
    begin = jnp.sum(onehot * starts[None, :], 1, dtype=jnp.int32)
    limit = jnp.sum(onehot * cached_lengths[None, :], 1, dtype=jnp.int32)
    group_of = jnp.sum(onehot * request_group[None, :], 1, dtype=jnp.int32)
    return (request, limit + token_ids - begin, group_of, limit)


def partial_softmax(scores, visible, value_block):
    allowed = visible[None, :, :]
    peak = jnp.max(jnp.where(allowed, scores, very_low), -1)
    weights = jnp.where(allowed, jnp.exp(scores - peak[..., None]), 0.0)
    total = jnp.sum(weights, -1)
    mixed = jnp.einsum(
        "hqk,khe->qhe",
        weights.astype(jnp.bfloat16),
        value_block,
        preferred_element_type=jnp.float32,
    )
    return (peak, total, mixed)


def combine(earlier, later):
    peak = jnp.maximum(earlier[0], later[0])
    scale_one = jnp.exp(earlier[0] - peak)
    scale_two = jnp.exp(later[0] - peak)
    total = earlier[1] * scale_one + later[1] * scale_two
    mixed = earlier[2] * scale_one.T[:, :, None] + later[2] * scale_two.T[:, :, None]
    return (peak, total, mixed)


def prefix_fold(running, cache_rows, query_block, query_group, query_limit, page_table):
    count = cache_rows.shape[0]
    stride = math.gcd(count, 8)
    heads_here = query_block.shape[1]
    per_prefix = page_table.shape[0] // GROUPS
    table_index = jnp.arange(page_table.shape[0], dtype=jnp.int32)

    def advance(turn_index, inner):
        block_rows = lax.dynamic_slice_in_dim(cache_rows, turn_index * stride, stride, 0)
        slots = turn_index * stride + jnp.arange(stride, dtype=jnp.int32)
        logical = jnp.sum(
            table_index[None, :] * (page_table[None, :] == slots[:, None]).astype(jnp.int32),
            1,
            dtype=jnp.int32,
        )
        key_group = jnp.repeat(logical // per_prefix, PAGE)
        key_position = (
            (logical % per_prefix)[:, None] * PAGE + jnp.arange(PAGE, dtype=jnp.int32)[None, :]
        ).reshape(-1)
        key_block = block_rows[:, :, 0].reshape(stride * PAGE, heads_here, HD)
        value_block = block_rows[:, :, 1].reshape(stride * PAGE, heads_here, HD)
        visible = (key_group[None, :] == query_group[:, None]) & (
            key_position[None, :] < query_limit[:, None]
        )
        scores = jnp.einsum(
            "qhe,khe->hqk", query_block, key_block, preferred_element_type=jnp.float32
        )
        return combine(inner, partial_softmax(scores, visible, value_block))

    return lax.fori_loop(0, count // stride, advance, running)


def attention_kernel(bounds_ref, q_ref, code_ref, pref_ref, win_ref, out_ref, m_ref, l_ref, acc_ref, *, steps):
    step = pl.program_id(0)
    width = q_ref.shape[1]

    @pl.when(step == 0)
    def _():
        m_ref[...] = jnp.full(m_ref.shape, very_low, jnp.float32)
        l_ref[...] = jnp.zeros(l_ref.shape, jnp.float32)
        acc_ref[...] = jnp.zeros(acc_ref.shape, jnp.float32)

    def fold(kv_ref, low, high):
        keys = kv_ref[:, :width]
        values = kv_ref[:, width:]
        scores = lax.dot_general(
            q_ref[...], keys, (((1,), (1,)), ((), ())), preferred_element_type=jnp.float32
        )
        code = code_ref[...]
        visible = (code >= low) & (code < high)
        peak_old = m_ref[...]
        peak = jnp.maximum(
            peak_old, jnp.max(jnp.where(visible, scores, very_low), axis=1, keepdims=True)
        )
        weights = jnp.where(visible, jnp.exp(scores - peak), 0.0)
        scale = jnp.exp(peak_old - peak)
        l_ref[...] = l_ref[...] * scale + jnp.sum(weights, axis=1, keepdims=True)
        acc_ref[...] = acc_ref[...] * scale + jnp.dot(
            weights.astype(jnp.bfloat16), values, preferred_element_type=jnp.float32
        )
        m_ref[...] = peak

    @pl.when(step < steps)
    def _():
        fold(pref_ref, bounds_ref[:, 0:1], bounds_ref[:, 1:2])

    @pl.when(step == steps)
    def _():
        fold(win_ref, bounds_ref[:, 2:3], bounds_ref[:, 3:4])
        out_ref[...] = (acc_ref[...] / l_ref[...]).astype(out_ref.dtype)


def attend(bounds, queries, codes, prefix_rows, window):
    rows, width = queries.shape
    block = window.shape[0]
    steps = prefix_rows.shape[0] // block
    keys_total = prefix_rows.shape[0] + block
    return pl.pallas_call(
        functools.partial(attention_kernel, steps=steps),
        out_shape=jax.ShapeDtypeStruct((rows, width), jnp.bfloat16),
        grid=(steps + 1,),
        in_specs=[
            pl.BlockSpec((rows, bounds.shape[1]), lambda i: (0, 0)),
            pl.BlockSpec((rows, width), lambda i: (0, 0)),
            pl.BlockSpec((1, block), lambda i: (0, i)),
            pl.BlockSpec((block, 2 * width), lambda i: (jnp.minimum(i, steps - 1), 0)),
            pl.BlockSpec((block, 2 * width), lambda i: (0, 0)),
        ],
        out_specs=pl.BlockSpec((rows, width), lambda i: (0, 0)),
        scratch_shapes=[
            pltpu.VMEM((rows, 1), jnp.float32),
            pltpu.VMEM((rows, 1), jnp.float32),
            pltpu.VMEM((rows, width), jnp.float32),
        ],
        compiler_params=pltpu.CompilerParams(dimension_semantics=("arbitrary",)),
        cost_estimate=pl.CostEstimate(
            flops=4 * rows * keys_total * width,
            transcendentals=rows * keys_total,
            bytes_accessed=2 * keys_total * 2 * width,
        ),
    )(bounds, queries, codes, prefix_rows, window)


def body(
    hidden_in,
    gain_attn,
    gain_mlp,
    w_qkv,
    w_up,
    w_out,
    w_down,
    prefix_cache,
    suffix_lengths,
    cached_lengths,
    request_group,
    page_table,
):
    row_count = hidden_in.shape[0]
    model_width = hidden_in.shape[1]
    row_total = lax.axis_size("row")
    col_total = lax.axis_size("col")
    row_place = lax.axis_index("row")
    col_place = lax.axis_index("col")
    head_width = w_qkv.shape[2]
    heads_here = head_width // HD
    normed = layer_normalize(hidden_in)
    attn_in = (normed * gain_attn).astype(jnp.bfloat16)
    mlp_in = (normed * gain_mlp).astype(jnp.bfloat16)
    rows_here = w_qkv.shape[0]
    qkv_columns = 3 * head_width
    joined = jnp.concatenate([w_qkv.reshape(rows_here, qkv_columns), w_up], 1)
    joined = lax.all_gather(joined, "row", axis=0, tiled=True)
    qkv_all = joined[:, :qkv_columns].reshape(model_width, 3, head_width)
    projected = jnp.einsum("td,dkh->tkh", attn_in, qkv_all, preferred_element_type=jnp.float32)
    up_sum = jnp.dot(mlp_in, joined[:, qkv_columns:], preferred_element_type=jnp.float32)
    token_total = row_total * row_count
    request_all, position_all, group_all, limit_all = token_table(
        suffix_lengths, cached_lengths, request_group, token_total
    )
    first_row = row_place * row_count
    local_request = lax.dynamic_slice_in_dim(request_all, first_row, row_count, 0)
    local_position = lax.dynamic_slice_in_dim(position_all, first_row, row_count, 0)
    local_group = lax.dynamic_slice_in_dim(group_all, first_row, row_count, 0)
    local_limit = lax.dynamic_slice_in_dim(limit_all, first_row, row_count, 0)
    projected = projected.reshape(row_count, 3, heads_here, HD)
    queries = (rotary(projected[:, 0], local_position) * HD ** (-0.5)).astype(jnp.bfloat16)
    keys_flat = (
        rotary(projected[:, 1], local_position).astype(jnp.bfloat16).reshape(row_count, head_width)
    )
    values_flat = projected[:, 2].astype(jnp.bfloat16).reshape(row_count, head_width)
    pair_rows = jnp.concatenate([keys_flat, values_flat], 1)
    previous = from_behind(pair_rows, "row", 1)
    window = jnp.concatenate([previous, pair_rows], 0)
    token_ids = first_row + jnp.arange(row_count, dtype=jnp.int32)
    local_begin = local_limit + token_ids - local_position
    prefix_span = 2 * page_table.shape[0] // GROUPS * PAGE
    bounds = jnp.stack(
        [
            local_group * prefix_span,
            local_group * prefix_span + local_limit,
            local_begin,
            token_ids + 1,
        ],
        1,
    )
    per_prefix = page_table.shape[0] // GROUPS
    slots = jnp.arange(page_table.shape[0], dtype=jnp.int32)
    logical = jnp.sum(
        slots[None, :] * (page_table[None, :] == slots[:, None]).astype(jnp.int32),
        1,
        dtype=jnp.int32,
    )
    slot_codes = (logical // per_prefix) * prefix_span + (logical % per_prefix) * PAGE
    prefix_codes = (slot_codes[:, None] + jnp.arange(PAGE, dtype=jnp.int32)[None, :]).reshape(-1)
    window_codes = first_row - row_count + jnp.arange(2 * row_count, dtype=jnp.int32)
    codes = jnp.concatenate([prefix_codes, window_codes])[None, :]
    cache_rows = prefix_cache.reshape(-1, 2 * head_width)
    prefix_rows = lax.all_gather(cache_rows, "row", axis=0, tiled=True)
    attention = attend(bounds, queries.reshape(row_count, head_width), codes, prefix_rows, window)
    activated = jax.nn.gelu(up_sum, approximate=False).astype(jnp.bfloat16)
    out_rows = w_out.shape[0]
    joined = jnp.concatenate([w_out.T, w_down.T], 1)
    joined = lax.all_gather(joined, "row", axis=0, tiled=True)
    contribution = jnp.einsum(
        "th,dh->td", attention, joined[:, :out_rows], preferred_element_type=jnp.float32
    ) + jnp.einsum("tf,df->td", activated, joined[:, out_rows:], preferred_element_type=jnp.float32)
    summed = lax.psum_scatter(
        contribution.astype(jnp.bfloat16), "col", scatter_dimension=1, tiled=True
    ).astype(jnp.float32)
    share = model_width // col_total
    residual = lax.dynamic_slice_in_dim(hidden_in, col_place * share, share, 1).astype(jnp.float32)
    return ((residual + summed).astype(jnp.bfloat16), keys_flat, values_flat)


def solution(mesh):
    in_specs = (
        P("row", None),
        P(),
        P(),
        P("row", None, "col"),
        P("row", "col"),
        P("col", "row"),
        P("col", "row"),
        P("row", None, None, "col"),
        P(),
        P(),
        P(),
        P(),
    )
    out_specs = (P("row", "col"), P("row", "col"), P("row", "col"))
    return jax.shard_map(body, mesh=mesh, in_specs=in_specs, out_specs=out_specs, check_vma=False)
```
